32 devices in a mesh: expert: 4 (over x, core), panel: 8 (over z, y).
Axes of the slice: x: 2, y: 2, z: 4, core: 2. Of those that a mesh axis runs over, the one named last changes fastest.
Arguments:
- activations: bfloat16 [2, 32, 96, 6144], P(None, ('expert', 'panel')), may hold values from -6 to 6
- gradients: bfloat16 [2, 32, 96, 16384], P(None, ('expert', 'panel')), may hold values from -6 to 6
- expert_ids: int32 [2, 32, 96, 1], P(None, ('expert', 'panel')), may hold values from 0 to 3; in each aligned block of 96 rows (0 to 95, 96 to 191, ..., all dimensions but the last counted through in order) at most 36 rows name the same one
- sequence_ids: int32 [2, 32, 96], P(None, ('expert', 'panel')), may hold values from 0 to 3, never falling along the last dimension, each value on 1 to 48 neighbouring positions
- input_basis: bfloat16 [4, 6144, 384], P('expert', 'panel'), may hold values from -0.078125 to 0.078125
- output_basis: bfloat16 [4, 16384, 256], P('expert', 'panel'), may hold values from -0.046875 to 0.046875
Outputs:
- corrected_eigenvalues: float32 [4, 384, 256], P('expert', 'panel')
The draws below stay inside these ranges and needn't reach their ends.
Inputs may be any that keep to these rules, and one draw needn't show every extreme that they name: `expert_ids`: among the 96 rows of one device block of one microbatch, no expert is named by more than 36 rows; some block names some expert exactly 36 times; every expert is named somewhere. `sequence_ids`: within a device block of one microbatch the numbers never fall, and each of the 4 sequences holds 1 to 48 rows.
All inputs are finite; a program needn't handle non-finite values.
Results may differ from the reference program's by a relative error of at most 0.00083.
Values may be sent and summed in bfloat16 or wider, within the bound.
No kernel may reach another device: no remote copies, remote signals or barrier semaphores. Data moves between devices by JAX's collectives and lax.ppermute only.
A program may use at most 128 MiB of HBM per device.

```python
import math
import jax
import jax.numpy as jnp
import numpy as np
from jax import lax

D = 6144
FF = 16384
EXPERTS = 4
KA = 384
KG = 256
MICRO = 2
SEQ_DEV = 4
TOK_DEV = 96
BLOCKS = 32
CAP = 36
N_EXPERT = 4
N_PANEL = 8


def steps_of(stream_key, dims, shards, smallest, high):
    factor_of, own = 1.0, jax.random.fold_in(stream_key, 6)
    for position, blocks in shards:
        draws = jnp.exp(jax.random.uniform(jax.random.fold_in(own, position), (blocks,), jnp.float32, smallest / len(shards), high / len(shards)))
        factor_of = factor_of * jnp.repeat(draws, dims[position] // blocks).reshape([-1 if axis == position else 1 for axis in range(len(dims))])
    return factor_of


def split_up(count, total, reach, slope):
    loads = [(1 << 20) // math.isqrt(rank ** slope) + 1 for rank in range(2, count + 1)]
    spare, counts = total - reach - (count - 1), [1] * (count - 1)
    while spare > 0:
        free = [i for i in range(count - 1) if counts[i] < reach]
        mass, left = sum([loads[i] for i in free]), spare
        for i in free:
            more = min(reach - counts[i], max(1, left * loads[i] // mass), spare)
            counts[i] = counts[i] + more
            spare = spare - more
    return np.array([reach] + counts)


def ragged(rng, amount, total, reach, skew):
    if amount == 2:
        one = jax.random.randint(rng, (), max(1, total - reach), min(reach, total - 1) + 1)
        return jnp.stack([one, total - one])
    sizes = jnp.asarray(split_up(amount, total, reach, skew), jnp.int32)
    twos = (amount - 1) // 2
    giver, taker = sizes[1:1 + 2 * twos:2], sizes[2:2 + 2 * twos:2]
    margin = jnp.minimum(giver - 1, reach - taker)
    moved = jax.random.randint(jax.random.fold_in(rng, 1), (twos,), 0, 1 << 20) % (margin + 1)
    sizes = sizes.at[1:1 + 2 * twos:2].set(giver - moved).at[2:2 + 2 * twos:2].set(taker + moved)
    return sizes[jax.random.permutation(jax.random.fold_in(rng, 2), amount)]


def routed_block(stream_key, own, number, rows, amount, top, reach, skew):
    ranking = jax.random.permutation(stream_key, amount)
    crowded, common = load_shares(amount, rows * top, reach, skew, True), load_shares(amount, rows * top, reach, skew, False)
    places = jnp.arange(amount)

    def named(tallies, rotation):
        used = int((tallies > 0).sum())
        fixed = max(1, used // 4)
        passed = fixed + (places - fixed + rotation * (used - fixed)) % max(1, amount - fixed)
        return jnp.zeros((amount,), jnp.int32).at[ranking[jnp.where(places < fixed, places, passed)]].set(jnp.asarray(tallies, jnp.int32))

    tallies = jnp.where(number % 4 == 0, named(crowded, number // 4), named(common, number - number // 4 - 1))
    mixed = jax.random.permutation(jax.random.fold_in(own, 3), amount)
    giver, receiver = mixed[0:amount // 2 * 2:2], mixed[1:amount // 2 * 2:2]
    room = jnp.minimum(tallies[giver] - 1, reach - tallies[receiver]) // 2
    room = jnp.where((giver == ranking[0]) | (receiver == ranking[0]) | (tallies[receiver] == 0), 0, jnp.maximum(room, 0))
    passed = jax.random.randint(jax.random.fold_in(own, 4), (amount // 2,), 0, 1 << 20) % (room + 1)
    tallies = tallies.at[giver].add(-passed).at[receiver].add(passed)
    members = jnp.searchsorted(jnp.cumsum(tallies), jnp.arange(rows * top), side="right").astype(jnp.int32)
    table = members.reshape(top, rows).T
    table = table[jax.random.permutation(jax.random.fold_in(own, 1), rows)]
    rotation = jax.random.randint(jax.random.fold_in(own, 2), (rows, 1), 0, top)
    return jnp.take_along_axis(table, (jnp.arange(top)[None, :] + rotation) % top, axis=1)


def load_shares(number_of, total, most, slope, full):
    loads = [(1 << 20) // math.isqrt(standing ** slope) + 1 for standing in range(1, number_of + 1)]
    largest = most if full else min(most, max(-(-total // number_of), total * loads[0] // sum(loads)))
    least = 1 if total - largest >= number_of - 1 else 0
    given, rest = [largest] + [least] * (number_of - 1), total - largest - least * (number_of - 1)
    while rest > 0:
        free = [i for i in range(1, number_of) if given[i] < largest] or [i for i in range(1, number_of) if given[i] < most]
        pool, remaining = sum([loads[i] for i in free]), rest
        for i in free:
            more = min(most - given[i], max(1, remaining * loads[i] // pool), rest)
            given[i] = given[i] + more
            rest = rest - more
    return np.array(given)


def scatter_about(rng, extent, width, limit, cuts=(), held_as=jnp.bfloat16):
    drawn = width * jax.random.normal(rng, extent, jnp.float32)
    if cuts:
        drawn = drawn * steps_of(rng, extent, cuts, -0.22, 0.18)
    return jnp.clip(drawn, -limit, limit).astype(held_as)


def setup_inputs(seed: int = 0) -> dict:
    arg_keys = jax.random.split(jax.random.key(seed), 7)
    activations = scatter_about(arg_keys[0], (MICRO, BLOCKS, TOK_DEV, D), 1.0, 6.0, ((1, 32),))
    gradients = scatter_about(arg_keys[1], (MICRO, BLOCKS, TOK_DEV, FF), 1.0, 6.0, ((1, 32),))
    expert_ids_keys = jax.random.split(jax.random.fold_in(arg_keys[2], 1), MICRO * BLOCKS * TOK_DEV // TOK_DEV)
    expert_ids_turns = jax.random.permutation(jax.random.fold_in(arg_keys[2], 3), MICRO * BLOCKS * TOK_DEV // TOK_DEV)
    expert_ids = jax.vmap(lambda own, number: routed_block(jax.random.fold_in(arg_keys[2], 2), own, number, TOK_DEV, EXPERTS, 1, CAP, 2))(expert_ids_keys, expert_ids_turns).reshape((MICRO, BLOCKS, TOK_DEV, 1))
    sequence_ids = jax.vmap(lambda own: jnp.searchsorted(jnp.cumsum(ragged(own, SEQ_DEV, TOK_DEV, TOK_DEV // 2, 1)), jnp.arange(TOK_DEV), side="right"))(jax.random.split(arg_keys[3], MICRO * BLOCKS)).reshape((MICRO, BLOCKS, TOK_DEV)).astype(jnp.int32)
    input_basis = scatter_about(arg_keys[4], (EXPERTS, D, KA), D ** -0.5, 0.078125, ((0, 4), (1, 8)))
    output_basis = scatter_about(arg_keys[5], (EXPERTS, FF, KG), FF ** -0.5, 0.046875, ((0, 4), (1, 8)))
    return {"activations": activations, "gradients": gradients, "expert_ids": expert_ids, "sequence_ids": sequence_ids, "input_basis": input_basis, "output_basis": output_basis}


def slots_for(inputs, grads, ids, seqs, expert, experts, capacity):
    tokens = ids.shape[0]
    onehot = (ids[:, None] == jnp.arange(experts, dtype=jnp.int32)[None, :]).astype(jnp.int32)
    before = jnp.cumsum(onehot, axis=0) - onehot
    offset = jnp.sum(before * onehot, axis=1).astype(jnp.int32)
    placed = (ids[:, None] == expert) & (offset[:, None] == jnp.arange(capacity, dtype=jnp.int32)[None, :])
    source = jnp.sum(jnp.where(placed, jnp.arange(tokens, dtype=jnp.int32)[:, None], 0), axis=0).astype(jnp.int32)
    filled = jnp.any(placed, axis=0)
    input_rows = jnp.where(filled[:, None], inputs[source], jnp.zeros((), inputs.dtype))
    grad_rows = jnp.where(filled[:, None], grads[source], jnp.zeros((), grads.dtype))
    labels = jnp.where(filled, seqs[source] + 1, 0).astype(jnp.int32)
    return input_rows, grad_rows, labels


def contract(rotated_inputs, rotated_grads, labels, seq_count):
    member = (labels[:, :, None] == jnp.arange(1, seq_count + 1, dtype=jnp.int32)[None, None, :]).astype(jnp.float32)
    masked = jnp.transpose(member, (0, 2, 1))[:, :, :, None] * rotated_inputs.astype(jnp.float32)[:, None, :, :]
    per_seq = jnp.einsum("sjca,scg->sjag", masked, rotated_grads.astype(jnp.float32), precision=lax.Precision.HIGHEST)
    return jnp.sum(per_seq * per_seq, axis=(0, 1))


def reference(activations, gradients, expert_ids, sequence_ids, input_basis, output_basis):
    total = jnp.zeros((EXPERTS, KA, KG), jnp.float32)
    for batch_index in range(MICRO):
        inputs = activations[batch_index]
        grads = gradients[batch_index]
        ids = expert_ids[batch_index, :, :, 0]
        seqs = sequence_ids[batch_index]

        def per_expert(packed):
            expert, basis_a, basis_g = packed
            input_rows, grad_rows, labels = jax.vmap(
                lambda one_in, one_grad, one_ids, one_seqs: slots_for(one_in, one_grad, one_ids, one_seqs, expert, EXPERTS, CAP)
            )(inputs, grads, ids, seqs)
            flat_in = input_rows.reshape(BLOCKS * CAP, D)
            flat_grad = grad_rows.reshape(BLOCKS * CAP, FF)
            rotated_in = jnp.dot(flat_in, basis_a, preferred_element_type=jnp.float32).astype(jnp.bfloat16)
            rotated_out = jnp.dot(flat_grad, basis_g, preferred_element_type=jnp.float32).astype(jnp.bfloat16)
            rotated_in = rotated_in.reshape(N_EXPERT, N_PANEL, CAP, KA)
            rotated_out = rotated_out.reshape(N_EXPERT, N_PANEL, CAP, KG)
            grouped = labels.reshape(N_EXPERT, N_PANEL, CAP)
            partial_sums = lax.map(lambda group: contract(group[0], group[1], group[2], SEQ_DEV), (rotated_in, rotated_out, grouped))
            return jnp.sum(partial_sums, axis=0)

        total = total + lax.map(per_expert, (jnp.arange(EXPERTS, dtype=jnp.int32), input_basis, output_basis))
    return total / (MICRO * BLOCKS * SEQ_DEV)
```

```python
import jax
import jax.numpy as jnp
from jax import lax
from jax.sharding import PartitionSpec as P

SEQ_DEV = 4
BF16 = jnp.bfloat16
F32 = jnp.float32


def ring_order(panels):
    inner = 1
    while inner * inner * 4 <= panels:
        inner *= 2
    while panels % inner:
        inner //= 2
    outer = panels // inner
    if inner < 2 or outer % 2:
        return list(range(panels))
    order = []
    for i in range(outer):
        columns = range(1, inner) if i % 2 == 0 else range(inner - 1, 0, -1)
        order += [i * inner + c for c in columns]
    return order + [i * inner for i in range(outer - 1, -1, -1)]


def gather_ring(block, order, index):
    n = len(order)
    right = [(order[i], order[(i + 1) % n]) for i in range(n)]
    left = [(order[i], order[i - 1]) for i in range(n)]
    table = jnp.asarray(order, jnp.int32)
    place = jnp.argmax(table == index)
    rows = block.shape[0]
    pieces = [(index, 0, block)]
    from_left = from_right = block
    for step in range(1, n // 2):
        from_left = lax.ppermute(from_left, "panel", right)
        from_right = lax.ppermute(from_right, "panel", left)
        pieces.append((table[(place - step) % n], 0, from_left))
        pieces.append((table[(place + step) % n], 0, from_right))
    half = rows // 2
    far = table[(place + n // 2) % n]
    pieces.append((far, 0, lax.ppermute(from_left[:half], "panel", right)))
    pieces.append((far, half, lax.ppermute(from_right[half:], "panel", left)))
    return pieces


def assemble(pieces, block_rows, panels):
    whole = jnp.zeros((block_rows * panels, pieces[0][2].shape[1]), pieces[0][2].dtype)
    for owner, offset, rows in pieces:
        whole = lax.dynamic_update_slice(whole, rows, (owner * block_rows + offset, 0))
    return whole


def contract(rotated_inputs, rotated_grads, labels):
    member = (
        labels[:, :, None] == jnp.arange(1, SEQ_DEV + 1, dtype=jnp.int32)[None, None, :]
    ).astype(BF16)
    masked = jnp.transpose(member, (0, 2, 1))[:, :, :, None] * rotated_inputs[:, None, :, :]
    per_seq = jnp.einsum("sjca,scg->sjag", masked, rotated_grads, preferred_element_type=F32)
    return jnp.sum(per_seq * per_seq, axis=(0, 1))


def per_device(activations, gradients, expert_ids, sequence_ids, input_basis, output_basis):
    experts = lax.axis_size("expert")
    panels = lax.axis_size("panel")
    me = lax.axis_index("expert")
    panel = lax.axis_index("panel")
    batches, _, tokens, width_in = activations.shape
    width_out = gradients.shape[3]
    capacity = tokens * 3 // (2 * experts)
    slots = batches * capacity
    order = ring_order(panels)

    in_pieces = gather_ring(input_basis[0], order, panel)
    out_pieces = gather_ring(output_basis[0], order, panel)

    inputs = activations.reshape(batches * tokens, width_in)
    grads = gradients.reshape(batches * tokens, width_out)
    ids = expert_ids[:, 0, :, 0]
    onehot = (ids[:, :, None] == jnp.arange(experts, dtype=jnp.int32)).astype(jnp.int32)
    before = jnp.cumsum(onehot, axis=1) - onehot
    offset = jnp.sum(before * onehot, axis=2)
    place = (offset + capacity * jnp.arange(batches, dtype=jnp.int32)[:, None]).reshape(-1)
    ids = ids.reshape(-1)
    seqs = sequence_ids[:, 0, :].reshape(-1)

    def swap(value, distance):
        if distance == 0:
            return value
        return lax.ppermute(value, "expert", [(i, i ^ distance) for i in range(experts)])

    def slots_of(distance):
        there = me ^ distance
        placed = (ids == there)[None, :] & (
            place[None, :] == jnp.arange(slots, dtype=jnp.int32)[:, None]
        )
        labels = jnp.sum(jnp.where(placed, seqs[None, :] + 1, 0), axis=1)
        return placed.astype(BF16), labels

    def pick(placed, rows):
        return jnp.dot(placed, rows, preferred_element_type=F32).astype(BF16)

    far_first = list(range(experts - 1, -1, -1))
    placed = {d: slots_of(d) for d in far_first}
    labels = jnp.stack([swap(placed[d][1], d) for d in range(experts)])
    in_rows = {d: swap(pick(placed[d][0], inputs), d) for d in far_first}
    half = width_out // 2
    grad_rows = {}
    for h in range(2):
        for d in far_first:
            grad_rows[d, h] = swap(pick(placed[d][0], grads[:, h * half : (h + 1) * half]), d)

    in_basis = assemble(in_pieces, input_basis.shape[1], panels)
    out_basis = assemble(out_pieces, output_basis.shape[1], panels)

    rotated_in = jnp.stack(
        [jnp.dot(in_rows[d], in_basis, preferred_element_type=F32).astype(BF16) for d in range(experts)]
    )
    rotated_out = jnp.stack(
        [
            (
                jnp.dot(grad_rows[d, 0], out_basis[:half], preferred_element_type=F32)
                + jnp.dot(grad_rows[d, 1], out_basis[half:], preferred_element_type=F32)
            ).astype(BF16)
            for d in range(experts)
        ]
    )
    blocks = experts * batches
    running = contract(
        rotated_in.reshape(blocks, capacity, -1),
        rotated_out.reshape(blocks, capacity, -1),
        labels.reshape(blocks, capacity),
    )
    parts = lax.all_to_all(
        running.reshape(panels, -1, running.shape[1]), "panel", split_axis=0, concat_axis=0, tiled=True
    )
    summed = jnp.sum(parts, axis=0)[None]
    return summed / (batches * experts * panels * SEQ_DEV)


def solution(mesh):
    placed = (
        P(None, ("expert", "panel"), None, None),
        P(None, ("expert", "panel"), None, None),
        P(None, ("expert", "panel"), None, None),
        P(None, ("expert", "panel"), None),
        P("expert", "panel", None),
        P("expert", "panel", None),
    )
    return jax.shard_map(
        per_device,
        mesh=mesh,
        in_specs=placed,
        out_specs=P("expert", "panel", None),
        check_vma=False,
    )
```
